128 devices in a mesh: dp: 32 (over x, z, core), mp: 4 (over y).
Axes of the slice: x: 4, y: 4, z: 4, core: 2. Of those that a mesh axis runs over, the one named last changes fastest.
Arguments:
- tokens: bfloat16 [8192, 1024], P('dp', 'mp'), may hold values from -6 to 6
- grad_out: bfloat16 [8192, 1024], P('dp', 'mp'), may hold values from -6 to 6
- gates: bfloat16 [8192, 2], P('dp'), may hold values from 0.099609375 to 0.8984375
- expert_ids: int32 [8192, 2], P('dp'), may hold values from 0 to 63, all different within a row; in each aligned block of 256 rows (0 to 255, 256 to 511, ...) at most 16 rows name the same one
- w_gate: bfloat16 [64, 1024, 4096], P('dp', None, 'mp'), may hold values from -0.1875 to 0.1875
- w_up: bfloat16 [64, 1024, 4096], P('dp', None, 'mp'), may hold values from -0.1875 to 0.1875
- w_down: bfloat16 [64, 4096, 1024], P('dp', 'mp'), may hold values from -0.09375 to 0.09375
Outputs:
- grad_tokens: bfloat16 [8192, 1024], P('dp', 'mp')
- grad_gates: float32 [8192, 2], P('dp')
- grad_w_gate: bfloat16 [64, 1024, 4096], P('dp', None, 'mp')
- grad_w_up: bfloat16 [64, 1024, 4096], P('dp', None, 'mp')
- grad_w_down: bfloat16 [64, 4096, 1024], P('dp', 'mp')
The draws below stay inside these ranges and needn't reach their ends.
Inputs may be any that keep to these rules, and one draw needn't show every extreme that they name: `expert_ids`: among the 256 tokens of one index of dp no expert is named more than 16 times, and in some such block some expert is named exactly 16 times; the two experts of a token differ.
All inputs are finite; a program needn't handle non-finite values.
Results may differ from the reference program's by a relative error of at most 0.0058.
Values may be sent and summed in bfloat16 or wider, within the bound.
A program may use at most 128 MiB of HBM per device.

```python
import math
import jax
import jax.numpy as jnp
import numpy as np
from jax import lax

D = 1024
FF = 4096
TOK_DEV = 256
EXPERTS = 64
CAP = 16
TOKENS = 8192
N_DP = 32


def levels(own_key, dims, pieces, least, largest):
    gain, own = 1.0, jax.random.fold_in(own_key, 6)
    for dim, shards_of in pieces:
        heights = jnp.exp(jax.random.uniform(jax.random.fold_in(own, dim), (shards_of,), jnp.float32, least / len(pieces), largest / len(pieces)))
        gain = gain * jnp.repeat(heights, dims[dim] // shards_of).reshape([-1 if axis == dim else 1 for axis in range(len(dims))])
    return gain


def shared_out(own_key, own, number, rows, number_of, top, bound, slope):
    sequence = jax.random.permutation(own_key, number_of)
    heavy_load, ordinary = load_shares(number_of, rows * top, bound, slope, True), load_shares(number_of, rows * top, bound, slope, False)
    places = jnp.arange(number_of)

    def named(tallies, rotation):
        used = int((tallies > 0).sum())
        fixed = max(1, used // 4)
        moved = fixed + (places - fixed + rotation * (used - fixed)) % max(1, number_of - fixed)
        return jnp.zeros((number_of,), jnp.int32).at[sequence[jnp.where(places < fixed, places, moved)]].set(jnp.asarray(tallies, jnp.int32))

    tallies = jnp.where(number % 4 == 0, named(heavy_load, number // 4), named(ordinary, number - number // 4 - 1))
    mixed = jax.random.permutation(jax.random.fold_in(own, 3), number_of)
    source_of, taker = mixed[0:number_of // 2 * 2:2], mixed[1:number_of // 2 * 2:2]
    slack = jnp.minimum(tallies[source_of] - 1, bound - tallies[taker]) // 2
    slack = jnp.where((source_of == sequence[0]) | (taker == sequence[0]) | (tallies[taker] == 0), 0, jnp.maximum(slack, 0))
    moved = jax.random.randint(jax.random.fold_in(own, 4), (number_of // 2,), 0, 1 << 20) % (slack + 1)
    tallies = tallies.at[source_of].add(-moved).at[taker].add(moved)
    labels = jnp.searchsorted(jnp.cumsum(tallies), jnp.arange(rows * top), side="right").astype(jnp.int32)
    grid = labels.reshape(top, rows).T
    grid = grid[jax.random.permutation(jax.random.fold_in(own, 1), rows)]
    rotation = jax.random.randint(jax.random.fold_in(own, 2), (rows, 1), 0, top)
    return jnp.take_along_axis(grid, (jnp.arange(top)[None, :] + rotation) % top, axis=1)


def load_shares(amount, total, reach, lean, full):
    weights = [(1 << 20) // math.isqrt(rank ** lean) + 1 for rank in range(1, amount + 1)]
    largest = reach if full else min(reach, max(-(-total // amount), total * weights[0] // sum(weights)))
    least = 1 if total - largest >= amount - 1 else 0
    given, rest = [largest] + [least] * (amount - 1), total - largest - least * (amount - 1)
    while rest > 0:
        free = [i for i in range(1, amount) if given[i] < largest] or [i for i in range(1, amount) if given[i] < reach]
        whole, left = sum([weights[i] for i in free]), rest
        for i in free:
            addition = min(reach - given[i], max(1, left * weights[i] // whole), rest)
            given[i] = given[i] + addition
            rest = rest - addition
    return np.array(given)


def centred(key, shape, spread, most, cuts=(), held_as=jnp.bfloat16):
    values = spread * jax.random.normal(key, shape, jnp.float32)
    if cuts:
        values = values * levels(key, shape, cuts, -0.22, 0.18)
    return jnp.clip(values, -most, most).astype(held_as)


def setup_inputs(seed: int = 0) -> dict:
    streams_of = jax.random.split(jax.random.key(seed), 8)
    tokens = centred(streams_of[0], (TOKENS, D), 1.0, 6.0, ((0, 32), (1, 4)))
    grad_out = centred(streams_of[1], (TOKENS, D), 1.0, 6.0, ((0, 32), (1, 4)))
    gates = jnp.clip(0.099609375 + 0.7988281 * jax.random.uniform(streams_of[2], (TOKENS, 2), jnp.float32) ** levels(streams_of[2], (TOKENS, 2), ((0, 32),), -0.2, 0.2), 0.099609375, 0.8984375).astype(jnp.bfloat16)
    expert_ids_keys = jax.random.split(jax.random.fold_in(streams_of[3], 1), TOKENS // TOK_DEV)
    expert_ids_turns = jax.random.permutation(jax.random.fold_in(streams_of[3], 3), TOKENS // TOK_DEV)
    expert_ids = jax.vmap(lambda own, number: shared_out(jax.random.fold_in(streams_of[3], 2), own, number, TOK_DEV, EXPERTS, 2, CAP, 2))(expert_ids_keys, expert_ids_turns).reshape((TOKENS, 2))
    w_gate = centred(streams_of[4], (EXPERTS, D, FF), D ** -0.5, 0.1875, ((0, 32), (2, 4)))
    w_up = centred(streams_of[5], (EXPERTS, D, FF), D ** -0.5, 0.1875, ((0, 32), (2, 4)))
    w_down = centred(streams_of[6], (EXPERTS, FF, D), FF ** -0.5, 0.09375, ((0, 32), (1, 4)))
    return dict(tokens=tokens, grad_out=grad_out, gates=gates, expert_ids=expert_ids, w_gate=w_gate, w_up=w_up, w_down=w_down)


def one_expert(inputs):
    rows_x, rows_dy, rows_gate, weight_gate, weight_up, weight_down = inputs
    gate_pre = jnp.dot(rows_x, weight_gate, preferred_element_type=jnp.float32)
    up_pre = jnp.dot(rows_x, weight_up, preferred_element_type=jnp.float32)
    sigmoid_gate = jax.nn.sigmoid(gate_pre)
    activated = gate_pre * sigmoid_gate
    hidden = (activated * up_pre).astype(jnp.bfloat16)
    output_rows = jnp.dot(hidden, weight_down, preferred_element_type=jnp.float32)
    gate_grad = jnp.sum(rows_dy.astype(jnp.float32) * output_rows, axis=1)
    scaled = (rows_gate.astype(jnp.float32)[:, None] * rows_dy.astype(jnp.float32)).astype(jnp.bfloat16)
    hidden_grad = jnp.dot(scaled, weight_down.T, preferred_element_type=jnp.float32)
    dgate = (hidden_grad * up_pre * sigmoid_gate * (1.0 + gate_pre * (1.0 - sigmoid_gate))).astype(jnp.bfloat16)
    dup = (hidden_grad * activated).astype(jnp.bfloat16)
    grad_down = jnp.dot(hidden.T, scaled, preferred_element_type=jnp.float32).astype(jnp.bfloat16)
    grad_gate = jnp.dot(rows_x.T, dgate, preferred_element_type=jnp.float32).astype(jnp.bfloat16)
    grad_up = jnp.dot(rows_x.T, dup, preferred_element_type=jnp.float32).astype(jnp.bfloat16)
    input_grad = (jnp.dot(dgate, weight_gate.T, preferred_element_type=jnp.float32)
                  + jnp.dot(dup, weight_up.T, preferred_element_type=jnp.float32))
    return grad_gate, grad_up, grad_down, input_grad, gate_grad


def reference(tokens, grad_out, gates, expert_ids, w_gate, w_up, w_down):
    onehot = (expert_ids[:, :, None] == jnp.arange(EXPERTS, dtype=jnp.int32)[None, None, :]).astype(jnp.int32)
    per_block = onehot.reshape(N_DP, TOK_DEV * 2, EXPERTS)
    before = jnp.cumsum(per_block, axis=1) - per_block
    position = jnp.sum(before * per_block, axis=2).reshape(TOKENS, 2)
    block_id = (jnp.arange(TOKENS, dtype=jnp.int32) // TOK_DEV)[:, None]
    slot = (block_id * CAP + position).astype(jnp.int32)
    total_rows = N_DP * CAP
    flat_expert = expert_ids.reshape(-1).astype(jnp.int32)
    flat_slot = slot.reshape(-1).astype(jnp.int32)
    buffer_x = jnp.zeros((EXPERTS, total_rows, D), tokens.dtype).at[flat_expert, flat_slot].set(jnp.repeat(tokens, 2, axis=0))
    buffer_dy = jnp.zeros((EXPERTS, total_rows, D), grad_out.dtype).at[flat_expert, flat_slot].set(jnp.repeat(grad_out, 2, axis=0))
    buffer_gate = jnp.zeros((EXPERTS, total_rows), gates.dtype).at[flat_expert, flat_slot].set(gates.reshape(-1))
    grad_gate, grad_up, grad_down, input_grad, gate_grad = lax.map(
        one_expert, (buffer_x, buffer_dy, buffer_gate, w_gate, w_up, w_down))
    picked = input_grad[flat_expert, flat_slot].reshape(TOKENS, 2, D)
    grad_tokens = jnp.sum(picked, axis=1).astype(jnp.bfloat16)
    grad_gates = gate_grad[flat_expert, flat_slot].reshape(TOKENS, 2)
    return grad_tokens, grad_gates, grad_gate, grad_up, grad_down
```

```python
import functools

import jax
import jax.numpy as jnp
from jax import lax
from jax.experimental import pallas as pl
from jax.experimental.pallas import tpu as pltpu
from jax.sharding import PartitionSpec as P

F32 = jnp.float32
BF16 = jnp.bfloat16
MESH = pl.DeviceIdType.MESH
RING = 4
GROUPS = 32
CAP = 16
LOCAL = 2
ROWS = GROUPS * CAP
TOK = 256
D = 1024
Q = 256
F = 1024
STEP = 256
PART = 128


def dot(a, b, contract):
    return lax.dot_general(a, b, ((contract[0], contract[1]), ((), ())), preferred_element_type=F32)


def peer(k, sign):
    me = lax.axis_index("dp")
    x, z, c = me // 8, (me // 2) % 4, me % 2
    dx, dz, dc = k // 8, (k // 2) % 4, k % 2
    x = (x + sign * dx + RING) % RING
    z = (z + sign * dz + RING) % RING
    c = (c + dc) % 2
    return x * 8 + z * 2 + c


def columns(q):
    return pl.ds(pl.multiple_of(q * Q, Q), Q)


def tile(j, size):
    return pl.ds(pl.multiple_of(j * size, size), size)


def local_wait(ref, sem):
    pltpu.make_async_copy(ref, ref, sem).wait()


def kernel(
    ids_ref, gates_ref, tokens_ref, dy_ref, wg_hbm, wu_hbm, wd_hbm,
    out_ref, gg_ref, gw_ref, uw_ref, dw_ref,
    wg, wu, wd, route, send, xs, pre_g, pre_u, pre_h, hid, dgate, dup,
    pa, pb, ra, rb, red, ret, back, gp, gt, gb, gl, gr, grad,
    w_sem, send_sem, a2a_sem, left_sem, right_sem, lf_sem, rf_sem,
    ra_sem, rb_sem, back_sem, gb_sem, gr_sem, out_sem,
):
    me = lax.axis_index("dp")
    y = lax.axis_index("mp")
    right, left, across = (y + 1) % RING, (y + 3) % RING, (y + 2) % RING
    barrier = pltpu.get_barrier_semaphore()

    def greet(k, _):
        pl.semaphore_signal(barrier, inc=1, device_id=(peer(k, 1), y), device_id_type=MESH)
        return 0

    lax.fori_loop(1, GROUPS, greet, 0)
    for other in (right, left, across):
        pl.semaphore_signal(barrier, inc=1, device_id=(me, other), device_id_type=MESH)

    loads = []
    for e in range(LOCAL):
        for i, (src, dst) in enumerate(((wg_hbm, wg), (wu_hbm, wu), (wd_hbm, wd))):
            copy = pltpu.make_async_copy(src.at[e], dst.at[e], w_sem.at[e, i])
            copy.start()
            loads.append(copy)

    expert_iota = lax.broadcasted_iota(jnp.int32, (LOCAL * GROUPS, TOK), 0)
    named = [(expert_iota == ids_ref[j : j + 1, :]).astype(F32) for j in range(2)]
    earlier = (
        lax.broadcasted_iota(jnp.int32, (TOK, TOK), 0) < lax.broadcasted_iota(jnp.int32, (TOK, TOK), 1)
    ).astype(F32)
    before = dot((named[0] + named[1]).astype(BF16), earlier.astype(BF16), ((1,), (0,)))
    x_me, z_me, c_me = me // 8, (me // 2) % 4, me % 2
    slot_iota = lax.broadcasted_iota(jnp.int32, (LOCAL * ROWS, TOK), 0)
    picks = []
    for j in range(2):
        position = jnp.sum(before * named[j], axis=0, keepdims=True).astype(jnp.int32)
        expert = ids_ref[j : j + 1, :]
        group = expert >> 1
        k = ((((group >> 3) - x_me) & 3) * 4 + ((((group >> 1) & 3) - z_me) & 3)) * 2 + (((group & 1) - c_me) & 1)
        slot = (expert & 1) * ROWS + k * CAP + position
        pick = (slot_iota == slot).astype(F32)
        route[j] = pick.astype(BF16)
        picks.append(pick)
    send_x = dot((picks[0] + picks[1]).astype(BF16), tokens_ref[...], ((1,), (0,)))
    weighted = (picks[0] * gates_ref[0:1, :] + picks[1] * gates_ref[1:2, :]).astype(BF16)
    send_s = dot(weighted, dy_ref[...], ((1,), (0,)))
    for e in range(LOCAL):
        send[0, e] = send_x[e * ROWS : (e + 1) * ROWS].astype(BF16)
        send[1, e] = send_s[e * ROWS : (e + 1) * ROWS].astype(BF16)

    pl.semaphore_wait(barrier, GROUPS - 1 + 3)

    own = columns(y)
    for e in range(LOCAL):
        pltpu.make_async_copy(
            send.at[:, e, pl.ds(0, CAP), :], xs.at[:, e, pl.ds(0, CAP), own], a2a_sem.at[e, 0]
        ).start()
        for g in range(RING):

            def dispatch(k, _):
                rows = tile(k, CAP)
                pltpu.make_async_remote_copy(
                    src_ref=send.at[:, e, rows, :],
                    dst_ref=xs.at[:, e, rows, own],
                    send_sem=send_sem.at[0],
                    recv_sem=a2a_sem.at[e, g],
                    device_id=(peer(k, 1), y),
                    device_id_type=MESH,
                ).start()
                return 0

            lax.fori_loop(max(1, g * 8), g * 8 + 8, dispatch, 0)

    def share(e, g):
        rows = pl.ds(g * PART, PART)
        local_wait(xs.at[:, e, rows, own], a2a_sem.at[e, g])
        for other, arrive, s in ((right, left_sem, 1), (left, right_sem, 2)):
            pltpu.make_async_remote_copy(
                src_ref=xs.at[:, e, rows, own],
                dst_ref=xs.at[:, e, rows, own],
                send_sem=send_sem.at[s],
                recv_sem=arrive.at[e, g],
                device_id=(me, other),
                device_id_type=MESH,
            ).start()

    def forward(e, g):
        rows = pl.ds(g * PART, PART)
        for origin, arrived, arrive, other, array, s in (
            (left, left_sem, lf_sem, right, 0, 3),
            (right, right_sem, rf_sem, left, 1, 4),
        ):
            cols = columns(origin)
            local_wait(xs.at[:, e, rows, cols], arrived.at[e, g])
            pltpu.make_async_remote_copy(
                src_ref=xs.at[array, e, rows, cols],
                dst_ref=xs.at[array, e, rows, cols],
                send_sem=send_sem.at[s],
                recv_sem=arrive.at[e, g],
                device_id=(me, other),
                device_id_type=MESH,
            ).start()

    def arrive_all(e):
        cols = columns(across)
        for g in range(RING):
            rows = pl.ds(g * PART, PART)
            local_wait(xs.at[0, e, rows, cols], lf_sem.at[e, g])
            local_wait(xs.at[1, e, rows, cols], rf_sem.at[e, g])

    def hidden_tiles(e, start, stop):
        def body(j, _):
            cols = tile(j, STEP)
            pre_g[...] = dot(xs[0, e], wg[e, :, cols], ((1,), (0,)))
            pre_u[...] = dot(xs[0, e], wu[e, :, cols], ((1,), (0,)))
            pre_h[...] = dot(xs[1, e], wd[e, cols, :], ((1,), (1,)))

            def rows_body(i, _):
                rows = tile(i, 64)
                g, u, dh = pre_g[rows, :], pre_u[rows, :], pre_h[rows, :]
                s = jax.nn.sigmoid(g)
                act = g * s
                h = (act * u).astype(BF16)
                hid[e, rows, cols] = h
                dgate[e, rows, cols] = (dh * u * s * (1.0 + g * (1.0 - s))).astype(BF16)
                dup[e, rows, cols] = (dh * act).astype(BF16)
                product = h.astype(F32) * dh
                gp[e, rows, :] += product[:, :128] + product[:, 128:]
                return 0

            lax.fori_loop(0, ROWS // 64, rows_body, 0)
            return 0

        lax.fori_loop(start, stop, body, 0)

    def dx_tile(e, q):
        rows = columns(q)
        return dot(dgate[e], wg[e, rows, :], ((1,), (1,))) + dot(dup[e], wu[e, rows, :], ((1,), (1,)))

    def ring_copy(src, dst, s, sem, other):
        pltpu.make_async_remote_copy(
            src_ref=src, dst_ref=dst, send_sem=send_sem.at[s], recv_sem=sem, device_id=(me, other), device_id_type=MESH
        ).start()

    half = ROWS // 2

    def reduce_first(e):
        pa[e] = dx_tile(e, across).astype(BF16)
        ring_copy(pa.at[e, pl.ds(0, half)], ra.at[e, 0], 5, ra_sem.at[e, 0], right)
        ring_copy(pa.at[e, pl.ds(half, half)], ra.at[e, 1], 5, ra_sem.at[e, 1], left)

    def reduce_second(e):
        pre_g[...] = dx_tile(e, right)
        local_wait(ra.at[e, 0], ra_sem.at[e, 0])
        pb[e, 0, :half] = (pre_g[:half] + ra[e, 0].astype(F32)).astype(BF16)
        pb[e, 0, half:] = pre_g[half:].astype(BF16)
        ring_copy(pb.at[e, 0], rb.at[e, 0], 6, rb_sem.at[e, 0], right)
        pre_g[...] = dx_tile(e, left)
        local_wait(ra.at[e, 1], ra_sem.at[e, 1])
        pb[e, 1, :half] = pre_g[:half].astype(BF16)
        pb[e, 1, half:] = (pre_g[half:] + ra[e, 1].astype(F32)).astype(BF16)
        ring_copy(pb.at[e, 1], rb.at[e, 1], 6, rb_sem.at[e, 1], left)
        red[e] = dx_tile(e, y)

    def give_back(e):
        local_wait(rb.at[e, 0], rb_sem.at[e, 0])
        local_wait(rb.at[e, 1], rb_sem.at[e, 1])
        ret[e] = (red[e] + rb[e, 0].astype(F32) + rb[e, 1].astype(F32)).astype(BF16)
        pltpu.make_async_copy(ret.at[e, pl.ds(0, CAP), :], back.at[e, pl.ds(0, CAP), :], back_sem.at[e]).start()

        def body(k, _):
            rows = tile(k, CAP)
            pltpu.make_async_remote_copy(
                src_ref=ret.at[e, rows, :],
                dst_ref=back.at[e, rows, :],
                send_sem=send_sem.at[7],
                recv_sem=back_sem.at[e],
                device_id=(peer(k, -1), y),
                device_id_type=MESH,
            ).start()
            return 0

        lax.fori_loop(1, GROUPS, body, 0)

    def weight_tiles(e, which, start, stop):
        rows_of, others, result, number = (
            (xs.at[0, e], dgate.at[e], gw_ref, 0),
            (xs.at[0, e], dup.at[e], uw_ref, 1),
            (hid.at[e], xs.at[1, e], dw_ref, 2),
        )[which]

        def body(j, _):
            cols = tile(j, STEP)
            grad[number, cols, :] = dot(rows_of[:, cols], others[...], ((0,), (0,))).astype(BF16)
            pltpu.make_async_copy(grad.at[number, cols, :], result.at[e, cols, :], out_sem.at[e, which]).start()
            return 0

        lax.fori_loop(start, stop, body, 0)

    def weights_wait(e):
        for which, result in enumerate((gw_ref, uw_ref, dw_ref)):
            local_wait(result.at[e], out_sem.at[e, which])

    def gates_back():
        lanes = lax.broadcasted_iota(jnp.int32, (ROWS, 128), 1)
        high, low = [], []
        for e in range(LOCAL):
            total = jnp.sum(gp[e], axis=1, keepdims=True)
            upper = total.astype(BF16).astype(F32)
            high.append(upper)
            low.append(total - upper)
        gt[...] = jnp.where(
            lanes < 32, high[0], jnp.where(lanes < 64, low[0], jnp.where(lanes < 96, high[1], low[1]))
        ).astype(BF16)
        pltpu.make_async_copy(gt.at[pl.ds(0, CAP), :], gb.at[pl.ds(0, CAP), :], gb_sem).start()

        def body(k, _):
            rows = tile(k, CAP)
            pltpu.make_async_remote_copy(
                src_ref=gt.at[rows, :],
                dst_ref=gb.at[rows, :],
                send_sem=send_sem.at[8],
                recv_sem=gb_sem,
                device_id=(peer(k, -1), y),
                device_id_type=MESH,
            ).start()
            return 0

        lax.fori_loop(1, GROUPS, body, 0)

    def gates_share():
        local_wait(gb, gb_sem)
        for j in range(2):
            first = dot(gb[...], route[j, :ROWS], ((0,), (0,)))
            second = dot(gb[...], route[j, ROWS:], ((0,), (0,)))
            gl[j : j + 1, :] = (first[0:1] + first[32:33]) + (second[64:65] + second[96:97])
        for i, other in enumerate((right, left, across)):
            ring_copy(gl, gr.at[i], 9, gr_sem.at[i], other)

    def gates_finish():
        for i in range(3):
            local_wait(gr.at[i], gr_sem.at[i])
        total = gl[0:2, :] + gr[0, 0:2, :] + gr[1, 0:2, :] + gr[2, 0:2, :]
        gg_ref[...] = total / gates_ref[...]

    gp[...] = jnp.zeros_like(gp)
    gl[...] = jnp.zeros_like(gl)

    for g in range(RING):
        share(0, g)
    for g in range(RING):
        forward(0, g)
    for g in range(RING):
        share(1, g)
    arrive_all(0)
    for copy in loads[:3]:
        copy.wait()
    hidden_tiles(0, 0, 3)
    forward(1, 0)
    hidden_tiles(0, 3, 4)
    reduce_first(0)
    weight_tiles(0, 0, 0, 2)
    forward(1, 1)
    reduce_second(0)
    forward(1, 2)
    weight_tiles(0, 0, 2, 4)
    weight_tiles(0, 1, 0, 4)
    forward(1, 3)
    give_back(0)
    weight_tiles(0, 2, 0, 4)
    arrive_all(1)
    for copy in loads[3:]:
        copy.wait()
    weights_wait(0)
    hidden_tiles(1, 0, 4)
    gates_back()
    reduce_first(1)
    weight_tiles(1, 0, 0, 2)
    reduce_second(1)
    gates_share()
    weight_tiles(1, 0, 2, 4)
    weight_tiles(1, 1, 0, 4)
    give_back(1)
    weight_tiles(1, 2, 0, 4)
    gates_finish()

    local_wait(back.at[0], back_sem.at[0])
    local_wait(back.at[1], back_sem.at[1])
    both = (route[0].astype(F32) + route[1].astype(F32)).astype(BF16)
    out_ref[...] = (
        dot(both[:ROWS], back[0], ((0,), (0,))) + dot(both[ROWS:], back[1], ((0,), (0,)))
    ).astype(BF16)

    weights_wait(1)
    local_wait(send.at[:, :, pl.ds(CAP, ROWS - CAP), :], send_sem.at[0])
    for s in (1, 2):
        local_wait(xs.at[:, :, :, own], send_sem.at[s])
    for s in (3, 4):
        local_wait(xs.at[0, :, :, own], send_sem.at[s])
    local_wait(pa, send_sem.at[5])
    local_wait(pb, send_sem.at[6])
    local_wait(ret.at[:, pl.ds(CAP, ROWS - CAP), :], send_sem.at[7])
    local_wait(gt.at[pl.ds(CAP, ROWS - CAP), :], send_sem.at[8])
    local_wait(gr, send_sem.at[9])


def on_device(tokens, grad_out, gates, expert_ids, w_gate, w_up, w_down):
    vmem = pl.BlockSpec(memory_space=pltpu.VMEM)
    hbm = pl.BlockSpec(memory_space=pl.ANY)
    weight = jax.ShapeDtypeStruct((LOCAL, D, F), BF16)
    dma = pltpu.SemaphoreType.DMA
    grad_tokens, grad_gates, grad_gate, grad_up, grad_down = pl.pallas_call(
        kernel,
        name="expert_layer",
        out_shape=(
            jax.ShapeDtypeStruct((TOK, Q), BF16),
            jax.ShapeDtypeStruct((2, TOK), F32),
            weight,
            weight,
            weight,
        ),
        in_specs=[vmem, vmem, vmem, vmem, hbm, hbm, hbm],
        out_specs=(vmem, vmem, hbm, hbm, hbm),
        scratch_shapes=[
            pltpu.VMEM((LOCAL, D, F), BF16),
            pltpu.VMEM((LOCAL, D, F), BF16),
            pltpu.VMEM((LOCAL, F, D), BF16),
            pltpu.VMEM((2, LOCAL * ROWS, TOK), BF16),
            pltpu.VMEM((2, LOCAL, ROWS, Q), BF16),
            pltpu.VMEM((2, LOCAL, ROWS, D), BF16),
            pltpu.VMEM((ROWS, STEP), F32),
            pltpu.VMEM((ROWS, STEP), F32),
            pltpu.VMEM((ROWS, STEP), F32),
            pltpu.VMEM((LOCAL, ROWS, F), BF16),
            pltpu.VMEM((LOCAL, ROWS, F), BF16),
            pltpu.VMEM((LOCAL, ROWS, F), BF16),
            pltpu.VMEM((LOCAL, ROWS, Q), BF16),
            pltpu.VMEM((LOCAL, 2, ROWS, Q), BF16),
            pltpu.VMEM((LOCAL, 2, ROWS // 2, Q), BF16),
            pltpu.VMEM((LOCAL, 2, ROWS, Q), BF16),
            pltpu.VMEM((LOCAL, ROWS, Q), F32),
            pltpu.VMEM((LOCAL, ROWS, Q), BF16),
            pltpu.VMEM((LOCAL, ROWS, Q), BF16),
            pltpu.VMEM((LOCAL, ROWS, 128), F32),
            pltpu.VMEM((ROWS, 128), BF16),
            pltpu.VMEM((ROWS, 128), BF16),
            pltpu.VMEM((8, TOK), F32),
            pltpu.VMEM((3, 8, TOK), F32),
            pltpu.VMEM((3, D, F), BF16),
            dma((LOCAL, 3)),
            dma((10,)),
            dma((LOCAL, RING)),
            dma((LOCAL, RING)),
            dma((LOCAL, RING)),
            dma((LOCAL, RING)),
            dma((LOCAL, RING)),
            dma((LOCAL, 2)),
            dma((LOCAL, 2)),
            dma((LOCAL,)),
            dma,
            dma((3,)),
            dma((LOCAL, 3)),
        ],
        compiler_params=pltpu.CompilerParams(
            collective_id=0, has_side_effects=True, vmem_limit_bytes=60 * 1024 * 1024
        ),
    )(expert_ids.T, gates.T.astype(F32), tokens, grad_out, w_gate, w_up, w_down)
    return grad_tokens, grad_gates.T, grad_gate, grad_up, grad_down


def solution(mesh):
    placed = (
        P("dp", "mp"),
        P("dp", "mp"),
        P("dp", None),
        P("dp", None),
        P("dp", None, "mp"),
        P("dp", None, "mp"),
        P("dp", "mp", None),
    )
    return jax.shard_map(
        on_device,
        mesh=mesh,
        in_specs=placed,
        out_specs=(
            P("dp", "mp"),
            P("dp", None),
            P("dp", None, "mp"),
            P("dp", None, "mp"),
            P("dp", "mp", None),
        ),
        check_vma=False,
    )
```

```python
import functools

import jax
import jax.numpy as jnp
from jax import lax
from jax.experimental import pallas as pl
from jax.experimental.pallas import tpu as pltpu
from jax.sharding import PartitionSpec as P

F32 = jnp.float32
BF16 = jnp.bfloat16
MESH = pl.DeviceIdType.MESH
RING = 4
GROUPS = 32
CAP = 16
LOCAL = 2
ROWS = GROUPS * CAP
TOK = 256
D = 1024
Q = 256
F = 1024
LANES = 128
STEP = 256
PART = 128


def dot(a, b, contract):
    return lax.dot_general(a, b, ((contract[0], contract[1]), ((), ())), preferred_element_type=F32)


def peer(k, sign):
    me = lax.axis_index("dp")
    x, z, c = me // 8, (me // 2) % 4, me % 2
    dx = (k // 2) % 4
    dz, dc = (dx + k // 8) % 4, k % 2
    x = (x + sign * dx + RING) % RING
    z = (z + sign * dz + RING) % RING
    c = (c + dc) % 2
    return x * 8 + z * 2 + c


def columns(q):
    return pl.ds(pl.multiple_of(q * Q, Q), Q)


def tile(j, size):
    return pl.ds(pl.multiple_of(j * size, size), size)


def local_wait(ref, sem):
    pltpu.make_async_copy(ref, ref, sem).wait()


def kernel(
    ids_ref, gates_ref, tokens_ref, dy_ref, wg_hbm, wu_hbm, wd_hbm,
    out_ref, gg_ref, gw_ref, uw_ref, dw_ref,
    wg, wu, wd, route, gated, late, early, dys, pan, sf, pre_g, pre_u, pre_h, hid, dgate, dup,
    pa, pb, ra, rb, red, ret, back, gp, gt, gb, gl, gr,
    w_sem, send_sem, late_sem, early_sem, dy_sem, left_sem, right_sem, lf_sem, rf_sem,
    ra_sem, rb_sem, back_sem, gb_sem, gr_sem,
):
    me = lax.axis_index("dp")
    y = lax.axis_index("mp")
    right, left, across = (y + 1) % RING, (y + 3) % RING, (y + 2) % RING
    barrier = pltpu.get_barrier_semaphore()

    def greet(k, _):
        pl.semaphore_signal(barrier, inc=1, device_id=(peer(k, 1), y), device_id_type=MESH)
        return 0

    lax.fori_loop(1, GROUPS, greet, 0)
    for other in (right, left, across):
        pl.semaphore_signal(barrier, inc=1, device_id=(me, other), device_id_type=MESH)

    loads = []
    for e in range(LOCAL):
        for i, (src, dst) in enumerate(((wg_hbm, wg), (wu_hbm, wu), (wd_hbm, wd))):
            copy = pltpu.make_async_copy(src.at[e], dst.at[e], w_sem.at[e, i])
            copy.start()
            loads.append(copy)

    gate_rows = gates_ref[...].astype(F32)
    expert_iota = lax.broadcasted_iota(jnp.int32, (LOCAL * GROUPS, TOK), 0)
    named = [(expert_iota == ids_ref[j : j + 1, :]).astype(F32) for j in range(2)]
    earlier = (
        lax.broadcasted_iota(jnp.int32, (TOK, TOK), 0) < lax.broadcasted_iota(jnp.int32, (TOK, TOK), 1)
    ).astype(F32)
    before = dot((named[0] + named[1]).astype(BF16), earlier.astype(BF16), ((1,), (0,)))
    x_me, z_me, c_me = me // 8, (me // 2) % 4, me % 2
    slot_iota = lax.broadcasted_iota(jnp.int32, (LOCAL * ROWS, TOK), 0)
    picks = []
    for j in range(2):
        position = jnp.sum(before * named[j], axis=0, keepdims=True).astype(jnp.int32)
        expert = ids_ref[j : j + 1, :]
        group = expert >> 1
        dx = ((group >> 3) - x_me) & 3
        dz = ((group >> 1) - z_me) & 3
        k = ((dz - dx) & 3) * 8 + dx * 2 + (((group & 1) - c_me) & 1)
        slot = (expert & 1) * ROWS + k * CAP + position
        pick = (slot_iota == slot).astype(F32)
        route[j] = pick.astype(BF16)
        picks.append(pick)
    send_x = dot((picks[0] + picks[1]).astype(BF16), tokens_ref[...], ((1,), (0,)))
    weighted = (picks[0] * gate_rows[0:1, :] + picks[1] * gate_rows[1:2, :]).astype(BF16)
    gated[...] = weighted
    send_s = dot(weighted, dy_ref[:, LANES:], ((1,), (0,)))
    for e in range(LOCAL):
        rows = slice(e * ROWS, (e + 1) * ROWS)
        late[e, 0] = send_x[rows, :LANES].astype(BF16)
        late[e, 1] = send_x[rows, LANES:].astype(BF16)
        late[e, 2] = send_s[rows].astype(BF16)

    pl.semaphore_wait(barrier, GROUPS - 1 + 3)

    def tokens_copy(src, origin, rows, sem, other):
        pltpu.make_async_remote_copy(
            src_ref=src,
            dst_ref=dys.at[origin, rows, :],
            send_sem=send_sem.at[10],
            recv_sem=sem,
            device_id=(me, other),
            device_id_type=MESH,
        ).start()

    everyone = pl.ds(0, TOK)
    pltpu.make_async_copy(dy_ref.at[:, pl.ds(0, LANES)], dys.at[y], dy_sem.at[0]).start()
    tokens_copy(dy_ref.at[:, pl.ds(0, LANES)], y, everyone, dy_sem.at[1], right)
    tokens_copy(dy_ref.at[:, pl.ds(0, LANES)], y, everyone, dy_sem.at[2], left)

    def send_late(e):
        pltpu.make_async_copy(
            late.at[e, :, pl.ds(0, CAP), :], pan.at[e, y, :, pl.ds(0, CAP), :], late_sem.at[e, 0]
        ).start()
        for g in range(RING):

            def body(k, _):
                rows = tile(k, CAP)
                pltpu.make_async_remote_copy(
                    src_ref=late.at[e, :, rows, :],
                    dst_ref=pan.at[e, y, :, rows, :],
                    send_sem=send_sem.at[0],
                    recv_sem=late_sem.at[e, g],
                    device_id=(peer(k, 1), y),
                    device_id_type=MESH,
                ).start()
                return 0

            lax.fori_loop(max(1, g * 8), g * 8 + 8, body, 0)

    def tokens_relay():
        local_wait(dys.at[left], dy_sem.at[1])
        lower = pl.ds(0, TOK // 2)
        tokens_copy(dys.at[left, lower, :], left, lower, dy_sem.at[3], right)
        local_wait(dys.at[right], dy_sem.at[2])
        upper = pl.ds(TOK // 2, TOK // 2)
        tokens_copy(dys.at[right, upper, :], right, upper, dy_sem.at[4], left)

    def route_early():
        local_wait(dys.at[y], dy_sem.at[0])
        local_wait(dys.at[across, pl.ds(0, TOK // 2), :], dy_sem.at[3])
        local_wait(dys.at[across, pl.ds(TOK // 2, TOK // 2), :], dy_sem.at[4])

        def body(q, _):
            rows = dot(gated[...], dys[q], ((1,), (0,)))
            for e in range(LOCAL):
                early[e, q] = rows[e * ROWS : (e + 1) * ROWS].astype(BF16)
            return 0

        lax.fori_loop(0, RING, body, 0)

    def send_early(e):
        pltpu.make_async_copy(
            early.at[e, :, pl.ds(0, CAP), :], sf.at[e, :, pl.ds(0, CAP), :], early_sem.at[e]
        ).start()

        def body(k, _):
            rows = tile(k, CAP)
            pltpu.make_async_remote_copy(
                src_ref=early.at[e, :, rows, :],
                dst_ref=sf.at[e, :, rows, :],
                send_sem=send_sem.at[11],
                recv_sem=early_sem.at[e],
                device_id=(peer(k, 1), y),
                device_id_type=MESH,
            ).start()
            return 0

        lax.fori_loop(1, GROUPS, body, 0)

    def share(e, g):
        rows = pl.ds(g * PART, PART)
        local_wait(pan.at[e, y, :, rows, :], late_sem.at[e, g])
        for other, arrive, s in ((right, left_sem, 1), (left, right_sem, 2)):
            pltpu.make_async_remote_copy(
                src_ref=pan.at[e, y, :, rows, :],
                dst_ref=pan.at[e, y, :, rows, :],
                send_sem=send_sem.at[s],
                recv_sem=arrive.at[e, g],
                device_id=(me, other),
                device_id_type=MESH,
            ).start()

    def forward(e, g):
        rows = pl.ds(g * PART, PART)
        cut = 2 - g % 2
        for origin, arrived, arrive, other, panels, s in (
            (left, left_sem, lf_sem, right, pl.ds(0, cut), 3),
            (right, right_sem, rf_sem, left, pl.ds(cut, 3 - cut), 4),
        ):
            local_wait(pan.at[e, origin, :, rows, :], arrived.at[e, g])
            pltpu.make_async_remote_copy(
                src_ref=pan.at[e, origin, panels, rows, :],
                dst_ref=pan.at[e, origin, panels, rows, :],
                send_sem=send_sem.at[s],
                recv_sem=arrive.at[e, g],
                device_id=(me, other),
                device_id_type=MESH,
            ).start()

    def arrive_all(e):
        for g in range(RING):
            rows = pl.ds(g * PART, PART)
            cut = 2 - g % 2
            local_wait(pan.at[e, across, pl.ds(0, cut), rows, :], lf_sem.at[e, g])
            local_wait(pan.at[e, across, pl.ds(cut, 3 - cut), rows, :], rf_sem.at[e, g])
        local_wait(sf.at[e], early_sem.at[e])

    def inputs(e):
        return jnp.concatenate([pan[e, q, i] for q in range(RING) for i in range(2)], axis=1)

    def scaled(e):
        return jnp.concatenate([part for q in range(RING) for part in (sf[e, q], pan[e, q, 2])], axis=1)

    def hidden_tiles(e, start, stop):
        def body(j, _):
            cols = tile(j, STEP)
            pre_g[...] = dot(inputs(e), wg[e, :, cols], ((1,), (0,)))
            pre_u[...] = dot(inputs(e), wu[e, :, cols], ((1,), (0,)))
            pre_h[...] = dot(scaled(e), wd[e, cols, :], ((1,), (1,)))

            def rows_body(i, _):
                rows = tile(i, 64)
                g, u, dh = pre_g[rows, :], pre_u[rows, :], pre_h[rows, :]
                s = jax.nn.sigmoid(g)
                act = g * s
                h = (act * u).astype(BF16)
                hid[e, rows, cols] = h
                dgate[e, rows, cols] = (dh * u * s * (1.0 + g * (1.0 - s))).astype(BF16)
                dup[e, rows, cols] = (dh * act).astype(BF16)
                product = h.astype(F32) * dh
                gp[e, rows, :] += product[:, :128] + product[:, 128:]
                return 0

            lax.fori_loop(0, ROWS // 64, rows_body, 0)
            return 0

        lax.fori_loop(start, stop, body, 0)

    def dx_tile(e, q):
        rows = columns(q)
        return dot(dgate[e], wg[e, rows, :], ((1,), (1,))) + dot(dup[e], wu[e, rows, :], ((1,), (1,)))

    def ring_copy(src, dst, s, sem, other):
        pltpu.make_async_remote_copy(
            src_ref=src, dst_ref=dst, send_sem=send_sem.at[s], recv_sem=sem, device_id=(me, other), device_id_type=MESH
        ).start()

    half = ROWS // 2

    def reduce_first(e):
        pa[e] = dx_tile(e, across).astype(BF16)
        ring_copy(pa.at[e, pl.ds(0, half)], ra.at[e, 0], 5, ra_sem.at[e, 0], right)
        ring_copy(pa.at[e, pl.ds(half, half)], ra.at[e, 1], 5, ra_sem.at[e, 1], left)

    def reduce_second(e):
        pre_g[...] = dx_tile(e, right)
        local_wait(ra.at[e, 0], ra_sem.at[e, 0])
        pb[e, 0, :half] = (pre_g[:half] + ra[e, 0].astype(F32)).astype(BF16)
        pb[e, 0, half:] = pre_g[half:].astype(BF16)
        ring_copy(pb.at[e, 0], rb.at[e, 0], 6, rb_sem.at[e, 0], right)
        pre_g[...] = dx_tile(e, left)
        local_wait(ra.at[e, 1], ra_sem.at[e, 1])
        pb[e, 1, :half] = pre_g[:half].astype(BF16)
        pb[e, 1, half:] = (pre_g[half:] + ra[e, 1].astype(F32)).astype(BF16)
        ring_copy(pb.at[e, 1], rb.at[e, 1], 6, rb_sem.at[e, 1], left)
        red[e] = dx_tile(e, y)

    def give_back(e):
        local_wait(rb.at[e, 0], rb_sem.at[e, 0])
        local_wait(rb.at[e, 1], rb_sem.at[e, 1])
        ret[e] = (red[e] + rb[e, 0].astype(F32) + rb[e, 1].astype(F32)).astype(BF16)
        pltpu.make_async_copy(ret.at[e, pl.ds(0, CAP), :], back.at[e, pl.ds(0, CAP), :], back_sem.at[e]).start()

        def body(k, _):
            rows = tile(k, CAP)
            pltpu.make_async_remote_copy(
                src_ref=ret.at[e, rows, :],
                dst_ref=back.at[e, rows, :],
                send_sem=send_sem.at[7],
                recv_sem=back_sem.at[e],
                device_id=(peer(k, -1), y),
                device_id_type=MESH,
            ).start()
            return 0

        lax.fori_loop(1, GROUPS, body, 0)

    def weight_tiles(e, which, start, stop):
        others, result = ((dgate, gw_ref), (dup, uw_ref), (None, dw_ref))[which]

        def body(j, _):
            cols = tile(j, STEP)
            if which == 2:
                result[e, cols, :] = dot(hid[e, :, cols], scaled(e), ((0,), (0,))).astype(BF16)
            else:
                rows_of = jnp.concatenate([pan[e, j, 0], pan[e, j, 1]], axis=1)
                result[e, cols, :] = dot(rows_of, others[e], ((0,), (0,))).astype(BF16)
            return 0

        lax.fori_loop(start, stop, body, 0)

    def gates_back():
        lanes = lax.broadcasted_iota(jnp.int32, (ROWS, 128), 1)
        high, low = [], []
        for e in range(LOCAL):
            total = jnp.sum(gp[e], axis=1, keepdims=True)
            upper = total.astype(BF16).astype(F32)
            high.append(upper)
            low.append(total - upper)
        gt[...] = jnp.where(
            lanes < 32, high[0], jnp.where(lanes < 64, low[0], jnp.where(lanes < 96, high[1], low[1]))
        ).astype(BF16)
        pltpu.make_async_copy(gt.at[pl.ds(0, CAP), :], gb.at[pl.ds(0, CAP), :], gb_sem).start()

        def body(k, _):
            rows = tile(k, CAP)
            pltpu.make_async_remote_copy(
                src_ref=gt.at[rows, :],
                dst_ref=gb.at[rows, :],
                send_sem=send_sem.at[8],
                recv_sem=gb_sem,
                device_id=(peer(k, -1), y),
                device_id_type=MESH,
            ).start()
            return 0

        lax.fori_loop(1, GROUPS, body, 0)

    def gates_share():
        local_wait(gb, gb_sem)
        for j in range(2):
            first = dot(gb[...], route[j, :ROWS], ((0,), (0,)))
            second = dot(gb[...], route[j, ROWS:], ((0,), (0,)))
            gl[j : j + 1, :] = (first[0:1] + first[32:33]) + (second[64:65] + second[96:97])
        for i, other in enumerate((right, left, across)):
            ring_copy(gl, gr.at[i], 9, gr_sem.at[i], other)

    def gates_finish():
        for i in range(3):
            local_wait(gr.at[i], gr_sem.at[i])
        total = gl[0:2, :] + gr[0, 0:2, :] + gr[1, 0:2, :] + gr[2, 0:2, :]
        gg_ref[...] = total / gate_rows

    gp[...] = jnp.zeros_like(gp)
    gl[...] = jnp.zeros_like(gl)

    send_late(0)
    tokens_relay()
    for g in range(RING):
        share(0, g)
    send_late(1)
    route_early()
    send_early(0)
    for g in range(RING):
        forward(0, g)
    for g in range(RING):
        share(1, g)
    send_early(1)
    arrive_all(0)
    for copy in loads[:3]:
        copy.wait()
    hidden_tiles(0, 0, 3)
    forward(1, 0)
    hidden_tiles(0, 3, 4)
    reduce_first(0)
    weight_tiles(0, 0, 0, 2)
    forward(1, 1)
    reduce_second(0)
    forward(1, 2)
    weight_tiles(0, 0, 2, 4)
    weight_tiles(0, 1, 0, 4)
    forward(1, 3)
    give_back(0)
    weight_tiles(0, 2, 0, 4)
    arrive_all(1)
    for copy in loads[3:]:
        copy.wait()
    hidden_tiles(1, 0, 4)
    gates_back()
    reduce_first(1)
    weight_tiles(1, 0, 0, 2)
    reduce_second(1)
    gates_share()
    weight_tiles(1, 0, 2, 4)
    weight_tiles(1, 1, 0, 4)
    give_back(1)
    weight_tiles(1, 2, 0, 4)
    gates_finish()

    local_wait(back.at[0], back_sem.at[0])
    local_wait(back.at[1], back_sem.at[1])
    both = (route[0].astype(F32) + route[1].astype(F32)).astype(BF16)
    out_ref[...] = (
        dot(both[:ROWS], back[0], ((0,), (0,))) + dot(both[ROWS:], back[1], ((0,), (0,)))
    ).astype(BF16)

    local_wait(late.at[:, :, pl.ds(CAP, ROWS - CAP), :], send_sem.at[0])
    for s in (1, 2):
        local_wait(pan.at[:, y], send_sem.at[s])
    for s in (3, 4):
        local_wait(pan.at[:, y, :, pl.ds(0, ROWS // 2), :], send_sem.at[s])
    local_wait(dys.at[pl.ds(0, 3)], send_sem.at[10])
    local_wait(early.at[:, :, pl.ds(CAP, ROWS - CAP), :], send_sem.at[11])
    local_wait(pa, send_sem.at[5])
    local_wait(pb, send_sem.at[6])
    local_wait(ret.at[:, pl.ds(CAP, ROWS - CAP), :], send_sem.at[7])
    local_wait(gt.at[pl.ds(CAP, ROWS - CAP), :], send_sem.at[8])
    local_wait(gr, send_sem.at[9])


def finish(*refs):
    count = len(refs) // 2
    sems = refs[-1]
    copies = []
    for i in range(count):
        for part in range(2 if i >= 2 else 1):
            src, dst = refs[i], refs[count + i]
            if i >= 2:
                src, dst = src.at[part], dst.at[part]
            copies.append(pltpu.make_async_copy(src, dst, sems.at[i, part]))
    for copy in copies:
        copy.start()
    for copy in copies:
        copy.wait()


def on_device(tokens, grad_out, gates, expert_ids, w_gate, w_up, w_down):
    vmem = pl.BlockSpec(memory_space=pltpu.VMEM)
    hbm = pl.BlockSpec(memory_space=pl.ANY)
    weight = pltpu.VMEM((LOCAL, D, F), BF16)
    dma = pltpu.SemaphoreType.DMA
    held = pl.pallas_call(
        kernel,
        name="expert_layer",
        out_shape=(
            pltpu.VMEM((TOK, Q), BF16),
            pltpu.VMEM((2, TOK), F32),
            weight,
            weight,
            weight,
        ),
        in_specs=[vmem, vmem, vmem, vmem, hbm, hbm, hbm],
        out_specs=(vmem, vmem, vmem, vmem, vmem),
        scratch_shapes=[
            pltpu.VMEM((LOCAL, D, F), BF16),
            pltpu.VMEM((LOCAL, D, F), BF16),
            pltpu.VMEM((LOCAL, F, D), BF16),
            pltpu.VMEM((2, LOCAL * ROWS, TOK), BF16),
            pltpu.VMEM((LOCAL * ROWS, TOK), BF16),
            pltpu.VMEM((LOCAL, 3, ROWS, LANES), BF16),
            pltpu.VMEM((LOCAL, RING, ROWS, LANES), BF16),
            pltpu.VMEM((RING, TOK, LANES), BF16),
            pltpu.VMEM((LOCAL, RING, 3, ROWS, LANES), BF16),
            pltpu.VMEM((LOCAL, RING, ROWS, LANES), BF16),
            pltpu.VMEM((ROWS, STEP), F32),
            pltpu.VMEM((ROWS, STEP), F32),
            pltpu.VMEM((ROWS, STEP), F32),
            pltpu.VMEM((LOCAL, ROWS, F), BF16),
            pltpu.VMEM((LOCAL, ROWS, F), BF16),
            pltpu.VMEM((LOCAL, ROWS, F), BF16),
            pltpu.VMEM((LOCAL, ROWS, Q), BF16),
            pltpu.VMEM((LOCAL, 2, ROWS, Q), BF16),
            pltpu.VMEM((LOCAL, 2, ROWS // 2, Q), BF16),
            pltpu.VMEM((LOCAL, 2, ROWS, Q), BF16),
            pltpu.VMEM((LOCAL, ROWS, Q), F32),
            pltpu.VMEM((LOCAL, ROWS, Q), BF16),
            pltpu.VMEM((LOCAL, ROWS, Q), BF16),
            pltpu.VMEM((LOCAL, ROWS, 128), F32),
            pltpu.VMEM((ROWS, 128), BF16),
            pltpu.VMEM((ROWS, 128), BF16),
            pltpu.VMEM((8, TOK), F32),
            pltpu.VMEM((3, 8, TOK), F32),
            dma((LOCAL, 3)),
            dma((12,)),
            dma((LOCAL, RING)),
            dma((LOCAL,)),
            dma((5,)),
            dma((LOCAL, RING)),
            dma((LOCAL, RING)),
            dma((LOCAL, RING)),
            dma((LOCAL, RING)),
            dma((LOCAL, 2)),
            dma((LOCAL, 2)),
            dma((LOCAL,)),
            dma,
            dma((3,)),
        ],
        compiler_params=pltpu.CompilerParams(
            collective_id=0, has_side_effects=True, vmem_limit_bytes=48 * 1024 * 1024
        ),
    )(expert_ids.T, gates.T, tokens, grad_out, w_gate, w_up, w_down)
    grad_tokens, grad_gates, grad_gate, grad_up, grad_down = pl.pallas_call(
        finish,
        name="finish",
        out_shape=[jax.ShapeDtypeStruct(a.shape, a.dtype) for a in held],
        in_specs=[hbm] * 5,
        out_specs=[hbm] * 5,
        scratch_shapes=[dma((5, 2))],
        compiler_params=pltpu.CompilerParams(vmem_limit_bytes=1024 * 1024),
    )(*held)
    return grad_tokens, grad_gates.T, grad_gate, grad_up, grad_down


def solution(mesh):
    placed = (
        P("dp", "mp"),
        P("dp", "mp"),
        P("dp", None),
        P("dp", None),
        P("dp", None, "mp"),
        P("dp", None, "mp"),
        P("dp", "mp", None),
    )
    return jax.shard_map(
        on_device,
        mesh=mesh,
        in_specs=placed,
        out_specs=(
            P("dp", "mp"),
            P("dp", None),
            P("dp", None, "mp"),
            P("dp", None, "mp"),
            P("dp", "mp", None),
        ),
        check_vma=False,
    )
```

```python
import functools

import jax
import jax.numpy as jnp
from jax import lax
from jax.experimental import pallas as pl
from jax.experimental.pallas import tpu as pltpu
from jax.sharding import PartitionSpec as P

F32 = jnp.float32
BF16 = jnp.bfloat16
MESH = pl.DeviceIdType.MESH
RING = 4
GROUPS = 32
CAP = 16
LOCAL = 2
ROWS = GROUPS * CAP
TOK = 256
D = 1024
Q = 256
F = 1024
LANES = 128
STEP = 256
HALF = 256
PART = 128


def dot(a, b, contract):
    return lax.dot_general(a, b, ((contract[0], contract[1]), ((), ())), preferred_element_type=F32)


def peer(k, sign):
    me = lax.axis_index("dp")
    x, z, c = me // 8, (me // 2) % 4, me % 2
    dx = (k // 2) % 4
    dz, dc = (dx + k // 8) % 4, k % 2
    x = (x + sign * dx + RING) % RING
    z = (z + sign * dz + RING) % RING
    c = (c + dc) % 2
    return x * 8 + z * 2 + c


def columns(q):
    return pl.ds(pl.multiple_of(q * Q, Q), Q)


def tile(j, size):
    return pl.ds(pl.multiple_of(j * size, size), size)


def local_wait(ref, sem):
    pltpu.make_async_copy(ref, ref, sem).wait()


def kernel(
    ids_ref, gates_ref, tokens_ref, dy_ref, wg_hbm, wu_hbm, wd_hbm,
    out_ref, gg_ref, gw_ref, uw_ref, dw_ref,
    wg, wu, wd, route, gated, late, early, dys, pan, sf, pre_g, pre_u, pre_h, hid, dgate, dup,
    pa, pb, ra, rb, red, ret, back, gp, gt, gb, gl, gr,
    w_sem, send_sem, late_sem, early_sem, dy_sem, left_sem, right_sem, lf_sem, rf_sem,
    ra_sem, rb_sem, back_sem, gb_sem, gr_sem,
):
    me = lax.axis_index("dp")
    y = lax.axis_index("mp")
    right, left, across = (y + 1) % RING, (y + 3) % RING, (y + 2) % RING
    barrier = pltpu.get_barrier_semaphore()

    def greet(k, _):
        pl.semaphore_signal(barrier, inc=1, device_id=(peer(k, 1), y), device_id_type=MESH)
        return 0

    lax.fori_loop(1, GROUPS, greet, 0)
    for other in (right, left, across):
        pl.semaphore_signal(barrier, inc=1, device_id=(me, other), device_id_type=MESH)

    loads = []
    for e in range(LOCAL):
        for i, (src, dst) in enumerate(((wg_hbm, wg), (wu_hbm, wu), (wd_hbm, wd))):
            copy = pltpu.make_async_copy(src.at[e], dst.at[e], w_sem.at[e, i])
            copy.start()
            loads.append(copy)

    gate_rows = gates_ref[...].astype(F32)
    expert_iota = lax.broadcasted_iota(jnp.int32, (LOCAL * GROUPS, TOK), 0)
    named = [(expert_iota == ids_ref[j : j + 1, :]).astype(F32) for j in range(2)]
    earlier = (
        lax.broadcasted_iota(jnp.int32, (TOK, TOK), 0) < lax.broadcasted_iota(jnp.int32, (TOK, TOK), 1)
    ).astype(F32)
    before = dot((named[0] + named[1]).astype(BF16), earlier.astype(BF16), ((1,), (0,)))
    x_me, z_me, c_me = me // 8, (me // 2) % 4, me % 2
    slot_iota = lax.broadcasted_iota(jnp.int32, (LOCAL * ROWS, TOK), 0)
    picks = []
    for j in range(2):
        position = jnp.sum(before * named[j], axis=0, keepdims=True).astype(jnp.int32)
        expert = ids_ref[j : j + 1, :]
        group = expert >> 1
        dx = ((group >> 3) - x_me) & 3
        dz = ((group >> 1) - z_me) & 3
        k = ((dz - dx) & 3) * 8 + dx * 2 + (((group & 1) - c_me) & 1)
        slot = (expert & 1) * ROWS + k * CAP + position
        pick = (slot_iota == slot).astype(F32)
        route[j] = pick.astype(BF16)
        picks.append(pick)
    send_x = dot((picks[0] + picks[1]).astype(BF16), tokens_ref[...], ((1,), (0,)))
    weighted = (picks[0] * gate_rows[0:1, :] + picks[1] * gate_rows[1:2, :]).astype(BF16)
    gated[...] = weighted
    send_s = dot(weighted, dy_ref[:, LANES:], ((1,), (0,)))
    for e in range(LOCAL):
        rows = slice(e * ROWS, (e + 1) * ROWS)
        late[e, 0] = send_x[rows, :LANES].astype(BF16)
        late[e, 1] = send_x[rows, LANES:].astype(BF16)
        late[e, 2] = send_s[rows].astype(BF16)

    pl.semaphore_wait(barrier, GROUPS - 1 + 3)

    def tokens_copy(src, origin, rows, sem, other):
        pltpu.make_async_remote_copy(
            src_ref=src,
            dst_ref=dys.at[origin, rows, :],
            send_sem=send_sem.at[10],
            recv_sem=sem,
            device_id=(me, other),
            device_id_type=MESH,
        ).start()

    everyone = pl.ds(0, TOK)
    pltpu.make_async_copy(dy_ref.at[:, pl.ds(0, LANES)], dys.at[y], dy_sem.at[0]).start()
    tokens_copy(dy_ref.at[:, pl.ds(0, LANES)], y, everyone, dy_sem.at[1], right)
    tokens_copy(dy_ref.at[:, pl.ds(0, LANES)], y, everyone, dy_sem.at[2], left)

    def send_late(e):
        pltpu.make_async_copy(
            late.at[e, :, pl.ds(0, CAP), :], pan.at[e, y, :, pl.ds(0, CAP), :], late_sem.at[e, 0]
        ).start()
        for g in range(RING):

            def body(k, _):
                rows = tile(k, CAP)
                pltpu.make_async_remote_copy(
                    src_ref=late.at[e, :, rows, :],
                    dst_ref=pan.at[e, y, :, rows, :],
                    send_sem=send_sem.at[0],
                    recv_sem=late_sem.at[e, g],
                    device_id=(peer(k, 1), y),
                    device_id_type=MESH,
                ).start()
                return 0

            lax.fori_loop(max(1, g * 8), g * 8 + 8, body, 0)

    def tokens_relay():
        local_wait(dys.at[left], dy_sem.at[1])
        lower = pl.ds(0, TOK // 2)
        tokens_copy(dys.at[left, lower, :], left, lower, dy_sem.at[3], right)
        local_wait(dys.at[right], dy_sem.at[2])
        upper = pl.ds(TOK // 2, TOK // 2)
        tokens_copy(dys.at[right, upper, :], right, upper, dy_sem.at[4], left)

    def route_early():
        local_wait(dys.at[y], dy_sem.at[0])
        local_wait(dys.at[across, pl.ds(0, TOK // 2), :], dy_sem.at[3])
        local_wait(dys.at[across, pl.ds(TOK // 2, TOK // 2), :], dy_sem.at[4])

        def body(q, _):
            rows = dot(gated[...], dys[q], ((1,), (0,)))
            for e in range(LOCAL):
                early[e, q] = rows[e * ROWS : (e + 1) * ROWS].astype(BF16)
            return 0

        lax.fori_loop(0, RING, body, 0)

    def send_early(e):
        pltpu.make_async_copy(
            early.at[e, :, pl.ds(0, CAP), :], sf.at[e, :, pl.ds(0, CAP), :], early_sem.at[e]
        ).start()

        def body(k, _):
            rows = tile(k, CAP)
            pltpu.make_async_remote_copy(
                src_ref=early.at[e, :, rows, :],
                dst_ref=sf.at[e, :, rows, :],
                send_sem=send_sem.at[11],
                recv_sem=early_sem.at[e],
                device_id=(peer(k, 1), y),
                device_id_type=MESH,
            ).start()
            return 0

        lax.fori_loop(1, GROUPS, body, 0)

    def share(e, g):
        rows = pl.ds(g * PART, PART)
        local_wait(pan.at[e, y, :, rows, :], late_sem.at[e, g])
        for other, arrive, s in ((right, left_sem, 1), (left, right_sem, 2)):
            pltpu.make_async_remote_copy(
                src_ref=pan.at[e, y, :, rows, :],
                dst_ref=pan.at[e, y, :, rows, :],
                send_sem=send_sem.at[s],
                recv_sem=arrive.at[e, g],
                device_id=(me, other),
                device_id_type=MESH,
            ).start()

    def forward(e, g):
        rows = pl.ds(g * PART, PART)
        cut = 2 - g % 2
        for origin, arrived, arrive, other, panels, s in (
            (left, left_sem, lf_sem, right, pl.ds(0, cut), 3),
            (right, right_sem, rf_sem, left, pl.ds(cut, 3 - cut), 4),
        ):
            local_wait(pan.at[e, origin, :, rows, :], arrived.at[e, g])
            pltpu.make_async_remote_copy(
                src_ref=pan.at[e, origin, panels, rows, :],
                dst_ref=pan.at[e, origin, panels, rows, :],
                send_sem=send_sem.at[s],
                recv_sem=arrive.at[e, g],
                device_id=(me, other),
                device_id_type=MESH,
            ).start()

    def arrive(e, h):
        for g in (2 * h, 2 * h + 1):
            rows = pl.ds(g * PART, PART)
            cut = 2 - g % 2
            local_wait(pan.at[e, across, pl.ds(0, cut), rows, :], lf_sem.at[e, g])
            local_wait(pan.at[e, across, pl.ds(cut, 3 - cut), rows, :], rf_sem.at[e, g])
        if h == 0:
            local_wait(sf.at[e], early_sem.at[e])

    def inputs(e, rows):
        return jnp.concatenate([pan[e, q, i, rows] for q in range(RING) for i in range(2)], axis=1)

    def scaled(e, rows):
        return jnp.concatenate([part for q in range(RING) for part in (sf[e, q, rows], pan[e, q, 2, rows])], axis=1)

    def hidden_tiles(e, h):
        chunk = slice(h * HALF, (h + 1) * HALF)

        def body(j, _):
            cols = tile(j, STEP)
            pre_g[...] = dot(inputs(e, chunk), wg[e, :, cols], ((1,), (0,)))
            pre_u[...] = dot(inputs(e, chunk), wu[e, :, cols], ((1,), (0,)))
            pre_h[...] = dot(scaled(e, chunk), wd[e, cols, :], ((1,), (1,)))

            def rows_body(i, _):
                near = tile(i, 64)
                rows = pl.ds(pl.multiple_of(h * HALF + i * 64, 64), 64)
                g, u, dh = pre_g[near, :], pre_u[near, :], pre_h[near, :]
                s = jax.nn.sigmoid(g)
                act = g * s
                value = (act * u).astype(BF16)
                hid[e, rows, cols] = value
                dgate[e, rows, cols] = (dh * u * s * (1.0 + g * (1.0 - s))).astype(BF16)
                dup[e, rows, cols] = (dh * act).astype(BF16)
                product = value.astype(F32) * dh
                gp[e, rows, :] += product[:, :128] + product[:, 128:]
                return 0

            lax.fori_loop(0, HALF // 64, rows_body, 0)
            return 0

        lax.fori_loop(0, F // STEP, body, 0)

    def dx_tile(e, h, q):
        chunk = slice(h * HALF, (h + 1) * HALF)
        rows = columns(q)
        return dot(dgate[e, chunk], wg[e, rows, :], ((1,), (1,))) + dot(dup[e, chunk], wu[e, rows, :], ((1,), (1,)))

    def ring_copy(src, dst, s, sem, other):
        pltpu.make_async_remote_copy(
            src_ref=src, dst_ref=dst, send_sem=send_sem.at[s], recv_sem=sem, device_id=(me, other), device_id_type=MESH
        ).start()

    def reduce_first(e, h):
        pa[e, h] = dx_tile(e, h, across).astype(BF16)
        ring_copy(pa.at[e, h, pl.ds(0, PART)], ra.at[e, h, 0], 5, ra_sem.at[e, h, 0], right)
        ring_copy(pa.at[e, h, pl.ds(PART, PART)], ra.at[e, h, 1], 5, ra_sem.at[e, h, 1], left)

    def reduce_second(e, h):
        part = dx_tile(e, h, right)
        local_wait(ra.at[e, h, 0], ra_sem.at[e, h, 0])
        pb[e, h, 0, :PART] = (part[:PART] + ra[e, h, 0].astype(F32)).astype(BF16)
        pb[e, h, 0, PART:] = part[PART:].astype(BF16)
        ring_copy(pb.at[e, h, 0], rb.at[e, h, 0], 6, rb_sem.at[e, h, 0], right)
        part = dx_tile(e, h, left)
        local_wait(ra.at[e, h, 1], ra_sem.at[e, h, 1])
        pb[e, h, 1, :PART] = part[:PART].astype(BF16)
        pb[e, h, 1, PART:] = (part[PART:] + ra[e, h, 1].astype(F32)).astype(BF16)
        ring_copy(pb.at[e, h, 1], rb.at[e, h, 1], 6, rb_sem.at[e, h, 1], left)
        red[e, h] = dx_tile(e, h, y)

    def give_back(e, h):
        local_wait(rb.at[e, h, 0], rb_sem.at[e, h, 0])
        local_wait(rb.at[e, h, 1], rb_sem.at[e, h, 1])
        ret[e, h * HALF : (h + 1) * HALF] = (
            red[e, h] + rb[e, h, 0].astype(F32) + rb[e, h, 1].astype(F32)
        ).astype(BF16)
        if h == 0:
            pltpu.make_async_copy(ret.at[e, pl.ds(0, CAP), :], back.at[e, pl.ds(0, CAP), :], back_sem.at[e]).start()

        def body(k, _):
            rows = tile(k, CAP)
            pltpu.make_async_remote_copy(
                src_ref=ret.at[e, rows, :],
                dst_ref=back.at[e, rows, :],
                send_sem=send_sem.at[7],
                recv_sem=back_sem.at[e],
                device_id=(peer(k, -1), y),
                device_id_type=MESH,
            ).start()
            return 0

        lax.fori_loop(1 if h == 0 else GROUPS // 2, GROUPS // 2 * (h + 1), body, 0)

    def weight_tiles(e, which, start, stop):
        others, result = ((dgate, gw_ref), (dup, uw_ref), (None, dw_ref))[which]

        def body(j, _):
            cols = tile(j, STEP)
            if which == 2:
                result[e, cols, :] = dot(hid[e, :, cols], scaled(e, slice(0, ROWS)), ((0,), (0,))).astype(BF16)
            else:
                rows_of = jnp.concatenate([pan[e, j, 0], pan[e, j, 1]], axis=1)
                result[e, cols, :] = dot(rows_of, others[e], ((0,), (0,))).astype(BF16)
            return 0

        lax.fori_loop(start, stop, body, 0)

    def gates_back():
        lanes = lax.broadcasted_iota(jnp.int32, (ROWS, 128), 1)
        high, low = [], []
        for e in range(LOCAL):
            total = jnp.sum(gp[e], axis=1, keepdims=True)
            upper = total.astype(BF16).astype(F32)
            high.append(upper)
            low.append(total - upper)
        gt[...] = jnp.where(
            lanes < 32, high[0], jnp.where(lanes < 64, low[0], jnp.where(lanes < 96, high[1], low[1]))
        ).astype(BF16)
        pltpu.make_async_copy(gt.at[pl.ds(0, CAP), :], gb.at[pl.ds(0, CAP), :], gb_sem).start()

        def body(k, _):
            rows = tile(k, CAP)
            pltpu.make_async_remote_copy(
                src_ref=gt.at[rows, :],
                dst_ref=gb.at[rows, :],
                send_sem=send_sem.at[8],
                recv_sem=gb_sem,
                device_id=(peer(k, -1), y),
                device_id_type=MESH,
            ).start()
            return 0

        lax.fori_loop(1, GROUPS, body, 0)

    def gates_share():
        local_wait(gb, gb_sem)
        for j in range(2):
            first = dot(gb[...], route[j, :ROWS], ((0,), (0,)))
            second = dot(gb[...], route[j, ROWS:], ((0,), (0,)))
            gl[j : j + 1, :] = (first[0:1] + first[32:33]) + (second[64:65] + second[96:97])
        for i, other in enumerate((right, left, across)):
            ring_copy(gl, gr.at[i], 9, gr_sem.at[i], other)

    def gates_finish():
        for i in range(3):
            local_wait(gr.at[i], gr_sem.at[i])
        total = gl[0:2, :] + gr[0, 0:2, :] + gr[1, 0:2, :] + gr[2, 0:2, :]
        gg_ref[...] = total / gate_rows

    gp[...] = jnp.zeros_like(gp)
    gl[...] = jnp.zeros_like(gl)

    send_late(0)
    tokens_relay()
    for g in range(RING):
        share(0, g)
    send_late(1)
    route_early()
    send_early(0)
    for g in range(RING):
        forward(0, g)
    for g in range(RING):
        share(1, g)
    send_early(1)
    arrive(0, 0)
    for copy in loads[:3]:
        copy.wait()
    hidden_tiles(0, 0)
    forward(1, 0)
    reduce_first(0, 0)
    forward(1, 1)
    arrive(0, 1)
    hidden_tiles(0, 1)
    forward(1, 2)
    reduce_first(0, 1)
    weight_tiles(0, 0, 0, 2)
    forward(1, 3)
    weight_tiles(0, 0, 2, 4)
    weight_tiles(0, 1, 0, 2)
    arrive(1, 0)
    for copy in loads[3:]:
        copy.wait()
    hidden_tiles(1, 0)
    reduce_first(1, 0)
    reduce_second(0, 0)
    reduce_second(0, 1)
    arrive(1, 1)
    hidden_tiles(1, 1)
    reduce_first(1, 1)
    gates_back()
    give_back(0, 0)
    give_back(0, 1)
    reduce_second(1, 0)
    weight_tiles(0, 1, 2, 4)
    reduce_second(1, 1)
    weight_tiles(0, 2, 0, 4)
    give_back(1, 0)
    gates_share()
    weight_tiles(1, 0, 0, 2)
    give_back(1, 1)
    weight_tiles(1, 0, 2, 4)
    weight_tiles(1, 1, 0, 4)
    weight_tiles(1, 2, 0, 4)
    gates_finish()

    both = (route[0].astype(F32) + route[1].astype(F32)).astype(BF16)
    local_wait(back.at[0], back_sem.at[0])
    first = dot(both[:ROWS], back[0], ((0,), (0,)))
    local_wait(back.at[1], back_sem.at[1])
    out_ref[...] = (first + dot(both[ROWS:], back[1], ((0,), (0,)))).astype(BF16)

    local_wait(late.at[:, :, pl.ds(CAP, ROWS - CAP), :], send_sem.at[0])
    for s in (1, 2):
        local_wait(pan.at[:, y], send_sem.at[s])
    for s in (3, 4):
        local_wait(pan.at[:, y, :, pl.ds(0, ROWS // 2), :], send_sem.at[s])
    local_wait(dys.at[pl.ds(0, 3)], send_sem.at[10])
    local_wait(early.at[:, :, pl.ds(CAP, ROWS - CAP), :], send_sem.at[11])
    local_wait(pa, send_sem.at[5])
    local_wait(pb, send_sem.at[6])
    local_wait(ret.at[:, pl.ds(CAP, ROWS - CAP), :], send_sem.at[7])
    local_wait(gt.at[pl.ds(CAP, ROWS - CAP), :], send_sem.at[8])
    local_wait(gr, send_sem.at[9])


def finish(*refs):
    count = len(refs) // 2
    sems = refs[-1]
    copies = []
    for i in range(count):
        for part in range(2 if i >= 2 else 1):
            src, dst = refs[i], refs[count + i]
            if i >= 2:
                src, dst = src.at[part], dst.at[part]
            copies.append(pltpu.make_async_copy(src, dst, sems.at[i, part]))
    for copy in copies:
        copy.start()
    for copy in copies:
        copy.wait()


def on_device(tokens, grad_out, gates, expert_ids, w_gate, w_up, w_down):
    vmem = pl.BlockSpec(memory_space=pltpu.VMEM)
    hbm = pl.BlockSpec(memory_space=pl.ANY)
    weight = pltpu.VMEM((LOCAL, D, F), BF16)
    dma = pltpu.SemaphoreType.DMA
    held = pl.pallas_call(
        kernel,
        name="expert_layer",
        out_shape=(
            pltpu.VMEM((TOK, Q), BF16),
            pltpu.VMEM((2, TOK), F32),
            weight,
            weight,
            weight,
        ),
        in_specs=[vmem, vmem, vmem, vmem, hbm, hbm, hbm],
        out_specs=(vmem, vmem, vmem, vmem, vmem),
        scratch_shapes=[
            pltpu.VMEM((LOCAL, D, F), BF16),
            pltpu.VMEM((LOCAL, D, F), BF16),
            pltpu.VMEM((LOCAL, F, D), BF16),
            pltpu.VMEM((2, LOCAL * ROWS, TOK), BF16),
            pltpu.VMEM((LOCAL * ROWS, TOK), BF16),
            pltpu.VMEM((LOCAL, 3, ROWS, LANES), BF16),
            pltpu.VMEM((LOCAL, RING, ROWS, LANES), BF16),
            pltpu.VMEM((RING, TOK, LANES), BF16),
            pltpu.VMEM((LOCAL, RING, 3, ROWS, LANES), BF16),
            pltpu.VMEM((LOCAL, RING, ROWS, LANES), BF16),
            pltpu.VMEM((HALF, STEP), F32),
            pltpu.VMEM((HALF, STEP), F32),
            pltpu.VMEM((HALF, STEP), F32),
            pltpu.VMEM((LOCAL, ROWS, F), BF16),
            pltpu.VMEM((LOCAL, ROWS, F), BF16),
            pltpu.VMEM((LOCAL, ROWS, F), BF16),
            pltpu.VMEM((LOCAL, 2, HALF, Q), BF16),
            pltpu.VMEM((LOCAL, 2, 2, HALF, Q), BF16),
            pltpu.VMEM((LOCAL, 2, 2, PART, Q), BF16),
            pltpu.VMEM((LOCAL, 2, 2, HALF, Q), BF16),
            pltpu.VMEM((LOCAL, 2, HALF, Q), F32),
            pltpu.VMEM((LOCAL, ROWS, Q), BF16),
            pltpu.VMEM((LOCAL, ROWS, Q), BF16),
            pltpu.VMEM((LOCAL, ROWS, 128), F32),
            pltpu.VMEM((ROWS, 128), BF16),
            pltpu.VMEM((ROWS, 128), BF16),
            pltpu.VMEM((8, TOK), F32),
            pltpu.VMEM((3, 8, TOK), F32),
            dma((LOCAL, 3)),
            dma((12,)),
            dma((LOCAL, RING)),
            dma((LOCAL,)),
            dma((5,)),
            dma((LOCAL, RING)),
            dma((LOCAL, RING)),
            dma((LOCAL, RING)),
            dma((LOCAL, RING)),
            dma((LOCAL, 2, 2)),
            dma((LOCAL, 2, 2)),
            dma((LOCAL,)),
            dma,
            dma((3,)),
        ],
        compiler_params=pltpu.CompilerParams(
            collective_id=0, has_side_effects=True, vmem_limit_bytes=48 * 1024 * 1024
        ),
    )(expert_ids.T, gates.T, tokens, grad_out, w_gate, w_up, w_down)
    grad_tokens, grad_gates, grad_gate, grad_up, grad_down = pl.pallas_call(
        finish,
        name="finish",
        out_shape=[jax.ShapeDtypeStruct(a.shape, a.dtype) for a in held],
        in_specs=[hbm] * 5,
        out_specs=[hbm] * 5,
        scratch_shapes=[dma((5, 2))],
        compiler_params=pltpu.CompilerParams(vmem_limit_bytes=1024 * 1024),
    )(*held)
    return grad_tokens, grad_gates.T, grad_gate, grad_up, grad_down


def solution(mesh):
    placed = (
        P("dp", "mp"),
        P("dp", "mp"),
        P("dp", None),
        P("dp", None),
        P("dp", None, "mp"),
        P("dp", None, "mp"),
        P("dp", "mp", None),
    )
    return jax.shard_map(
        on_device,
        mesh=mesh,
        in_specs=placed,
        out_specs=(
            P("dp", "mp"),
            P("dp", None),
            P("dp", None, "mp"),
            P("dp", None, "mp"),
            P("dp", "mp", None),
        ),
        check_vma=False,
    )
```
